32 devices in a mesh: col: 8 (over y, x, core), row: 4 (over z).
Axes of the slice: x: 2, y: 2, z: 4, core: 2. Of those that a mesh axis runs over, the one named last changes fastest.
Arguments:
- rhs: bfloat16 [6, 8, 4, 128, 512], P(None, 'col', 'row'), may hold values from -6 to 6
- diag_inv: bfloat16 [6, 8, 4, 128, 128], P(None, 'col', 'row'), may hold values from -0.5 to 0.5
- factor: bfloat16 [5, 8, 4, 8, 2, 128, 128], P(None, 'col', 'row'), may hold values from -0.1875 to 0.1875
- columns: int32 [5, 8, 4, 8, 2], P(None, 'col', 'row'), may hold values from 0 to 3, as said below
Outputs:
- solution: bfloat16 [6, 8, 4, 128, 512], P(None, 'col', 'row')
The draws below stay inside these ranges and needn't reach their ends.
Inputs may be any that keep to these rules, and one draw needn't show every extreme that they name: The 2 entries of columns for one factor row block and one column owner are distinct.
All inputs are finite; a program needn't handle non-finite values.
Results may differ from the reference program's by a relative error of at most 0.025.
Values may be sent and summed in bfloat16 or wider, within the bound.
A program may use at most 128 MiB of HBM per device.

```python
import jax
import jax.numpy as jnp
from jax import lax

BLK = 128
NRHS = 512
STEPS = 6
SLOTS = 2
N_COL = 8
N_ROW = 4


def draw_columns(key, part):
    shape = (STEPS - 1, N_COL, N_ROW, N_COL, N_ROW)
    scores = jax.random.randint(jax.random.fold_in(key, 17), shape, 0, 1000)
    scores = scores * N_ROW + jnp.arange(N_ROW, dtype=jnp.int32)
    order = jnp.argsort(scores, axis=-1)
    return order[..., :SLOTS].astype(jnp.int32)


def spiked(result, stream_key, source, target, parts, factor):
    owner, partner = [(jnp.arange(result.shape[dim]) // (result.shape[dim] // parts)).reshape([-1 if axis == dim else 1 for axis in range(result.ndim)]) for dim in (source, target)]
    chosen = jax.random.permutation(stream_key, parts)[partner]
    strong = (owner == chosen) | (owner == (partner + parts // 2) % parts)
    return jnp.where(strong, factor * result, result)


def levels(stream_key, dims, shards, low, largest):
    level = 1.0
    for position, parts in shards:
        steps = jax.random.uniform(jax.random.fold_in(jax.random.fold_in(stream_key, 6), position), (parts,), jnp.float32, low / len(shards), largest / len(shards))
        level = level * jnp.repeat(jnp.exp(steps), dims[position] // parts).reshape((-1,) + (1,) * (len(dims) - 1 - position))
    return level


def gaussian(rng, extent, spread, most, split=(), kind=jnp.bfloat16):
    loudness = levels(rng, extent, split, -0.22, 0.18) if split else 1.0
    array = jax.random.normal(rng, extent, jnp.float32) * spread * loudness
    return jnp.minimum(jnp.maximum(array, -most), most).astype(kind)


def bell_draw_with(stream_key, dims, spread, bound, shards, heavy, held_as=jnp.bfloat16):
    entries = spread * jax.random.normal(stream_key, dims, jnp.float32)
    if shards:
        entries = entries * levels(stream_key, dims, shards, -0.22, 0.18)
    return jnp.clip(spiked(entries, jax.random.fold_in(stream_key, 3), *heavy), -bound, bound).astype(held_as)


def setup_inputs(seed: int = 0) -> dict:
    key_of = jax.random.split(jax.random.key(seed), 5)
    return {
        "rhs": gaussian(key_of[0], (STEPS, N_COL, N_ROW, BLK, NRHS), 1.0, 6.0, ((1, 8), (2, 4))),
        "diag_inv": gaussian(key_of[1], (STEPS, N_COL, N_ROW, BLK, BLK), BLK ** -0.5, 0.5, ((1, 8), (2, 4))),
        "factor": bell_draw_with(key_of[2], (STEPS - 1, N_COL, N_ROW, N_COL, SLOTS, BLK, BLK), (N_COL * SLOTS * BLK) ** -0.5, 0.1875, ((1, 8), (2, 4)), (1, 3, 8, 2.0)),
        "columns": draw_columns(jax.random.fold_in(key_of[4], 71), 0),
    }


def reference(rhs, diag_inv, factor, columns):
    highest = lax.Precision.HIGHEST
    remainder = rhs[0].astype(jnp.float32)
    solved = []
    for step_index in range(STEPS):
        current = jnp.einsum('crab,crbn->cran', diag_inv[step_index].astype(jnp.float32), remainder, precision=highest).astype(jnp.bfloat16)
        solved.append(current)
        if step_index + 1 < STEPS:
            def add_owner(carry, inputs):
                blocks, selected, panels = inputs
                chosen = jnp.take(panels, selected, axis=0).astype(jnp.float32)
                part_sum = jnp.einsum('rtmab,rtmbn->rtan', blocks.astype(jnp.float32), chosen, precision=highest)
                rounded = lax.optimization_barrier(part_sum.astype(jnp.bfloat16))
                return carry + rounded.astype(jnp.float32), None

            start_sum = jnp.zeros((N_ROW, N_COL, BLK, NRHS), jnp.float32)
            total, unused = lax.scan(add_owner, start_sum, (factor[step_index], columns[step_index], current))
            remainder = rhs[step_index + 1].astype(jnp.float32) - jnp.transpose(total, (1, 0, 2, 3))
    return jnp.stack(solved)
```

```python
import functools

import jax
import jax.numpy as jnp
from jax import lax
from jax.experimental import pallas as pl
from jax.experimental.pallas import tpu as pltpu
from jax.sharding import PartitionSpec as P

MESH = pl.DeviceIdType.MESH
CHUNKS = 4
LAG = 1.5
EARLY = 1.2
RELAY = "none"


def relay_ways(n_row, s, ch):
    if n_row < 4 or s == 0 or RELAY == "none":
        return ()
    if RELAY == "both":
        return (-1, 1)
    return (-1,) if ch % 2 == 0 else (1,)


def kernel(n_col, n_row, rhs, diag, fac, cols, cols_hbm, out, *scratch):
    steps, rows, width = rhs.shape[0], rhs.shape[3], rhs.shape[4]
    slots = fac.shape[4]
    chips = n_col // 2
    half = width // 2
    wide = half // CHUNKS
    fold = max(1, 128 // wide)
    tall = rows // fold
    links = steps - 1
    reach = [sign * h for h in range(n_row - 1, 0, -1) for sign in (-1, 1)]

    (first, away, rv, dv, fv, cp, own, sent, landed, stage,
     f_loc, in_loc, in_send, in_recv, a_send, a_recv, z_send, z_recv, y_send,
     c_send, c_recv, o_loc, o_send, o_recv) = scratch[:24]
    panels = scratch[24:]

    col = lax.axis_index("col")
    row = lax.axis_index("row")
    core = lax.rem(col, 2)
    chip = lax.div(col, 2)
    partner = col + 1 - 2 * core
    mine = pl.ds(pl.multiple_of(core * half, half), half)
    theirs = pl.ds(pl.multiple_of((1 - core) * half, half), half)

    def to(c, r):
        return {"col": c, "row": r}

    def reaches(step):
        return (row + step >= 0) & (row + step < n_row)

    def shifted(d):
        y = lax.rem(lax.div(chip, 2) + lax.div(d, 2), max(1, chips // 2))
        x = lax.rem(lax.rem(chip, 2) + lax.rem(d, 2), 2)
        return y * 2 + x

    barrier = pltpu.get_barrier_semaphore()

    def greet(c, r):
        pl.semaphore_signal(barrier, inc=1, device_id=to(c, r), device_id_type=MESH)

    count = chips
    for step in reach:
        count = count + 2 * reaches(step).astype(jnp.int32)

        @pl.when(reaches(step))
        def _():
            greet(col, row + step)
            greet(partner, row + step)

    for d in range(1, chips):
        greet(shifted(d) * 2 + core, row)
    greet(partner, row)

    start = [
        pltpu.make_async_copy(diag.at[0, 0, 0], dv.at[0, 0], f_loc.at[0]),
        pltpu.make_async_copy(rhs.at[0, 0, 0, :, mine], first.at[0], f_loc.at[1]),
        pltpu.make_async_copy(rhs.at[0, 0, 0, :, theirs], first.at[1], f_loc.at[2]),
    ]
    for c in start:
        c.start()
    later = pl.ds(1, links)
    zero, rest = pl.ds(0, 1), pl.ds(1, links - 1)
    local = {
        "rhs": pltpu.make_async_copy(rhs.at[later, 0, 0, :, mine], rv.at[:, 0], in_loc.at[0]),
        "diag": pltpu.make_async_copy(diag.at[later, 0, 0], dv.at[later, 0], in_loc.at[1]),
        "fac0": pltpu.make_async_copy(fac.at[zero, 0, 0], fv.at[zero, 0], in_loc.at[2]),
        "fac": pltpu.make_async_copy(fac.at[rest, 0, 0], fv.at[rest, 0], in_loc.at[3]),
    }
    for name in ("fac0", "rhs", "diag", "fac"):
        local[name].start()

    def pack(x):
        return x if fold == 1 else jnp.concatenate(
            [x[i * tall:(i + 1) * tall] for i in range(fold)], axis=1)

    def unpack(x):
        return x if fold == 1 else jnp.concatenate(
            [x[:, i * wide:(i + 1) * wide] for i in range(fold)], axis=0)

    def part(ch):
        return pl.ds(ch * wide, wide)

    for c in start:
        c.wait()
    for k in range(2):
        x = jnp.dot(dv[0, 0], first[k], preferred_element_type=jnp.float32).astype(jnp.bfloat16)
        stage[0, k] = x
        for ch in range(CHUNKS):
            piece = pack(x[:, ch * wide:(ch + 1) * wide])
            if k == 0:
                panels[ch][row, 0] = piece
            else:
                away[ch] = piece
    pl.semaphore_wait(barrier, count)

    def remote(src, dst, send, recv, device):
        return pltpu.make_async_remote_copy(
            src_ref=src, dst_ref=dst, send_sem=send, recv_sem=recv,
            device_id=device, device_id_type=MESH)

    def open_copy(ch, k, step):
        way = n_row - 1 + step
        source = panels[ch].at[row, 0] if k == 0 else away.at[ch]
        return remote(source, panels[ch].at[row, k], a_send.at[ch, k, way],
                      a_recv.at[ch, k, row], to(col if k == 0 else partner, row + step))

    def open_wait(ch, k, step):
        remote(panels[ch].at[row + step, k], panels[ch].at[row + step, k], a_send.at[ch, k, 0],
               a_recv.at[ch, k, row + step], to(col, row)).wait_recv()

    for ch in range(CHUNKS):
        for step in reach:
            @pl.when(reaches(step))
            def _():
                for k in range(2):
                    open_copy(ch, k, step).start()
        open_copy(ch, 1, 0).start()

    pair = to(partner, row)
    cross = {
        "cols": remote(cols_hbm, cp, in_send.at[4], in_recv.at[4], pair),
        "fac0": remote(fac.at[zero, 0, 0], fv.at[zero, 1], in_send.at[2], in_recv.at[2], pair),
        "rhs": remote(rhs.at[later, 0, 0, :, theirs], rv.at[:, 1], in_send.at[0], in_recv.at[0], pair),
        "diag": remote(diag.at[later, 0, 0], dv.at[later, 1], in_send.at[1], in_recv.at[1], pair),
        "fac": remote(fac.at[rest, 0, 0], fv.at[rest, 1], in_send.at[3], in_recv.at[3], pair),
    }
    for c in cross.values():
        c.start()

    def arrived(name):
        if name in local:
            local[name].wait()
        cross[name].wait_recv()

    def ways(s, ch):
        return relay_ways(n_row, s, ch)

    def source_of(way):
        return n_row // 2 if way < 0 else n_row // 2 - 1

    def goes(s, ch, step):
        ok = reaches(step)
        for way in ways(s, ch):
            if step == 2 * way:
                ok = ok & (row != source_of(way))
        return ok

    def z_copy(s, ch, step):
        buf = panels[s * CHUNKS + ch]
        return remote(buf.at[row], buf.at[row], z_send.at[s, ch, n_row - 1 + step],
                      z_recv.at[s, ch, row], to(col, row + step))

    def z_wait(s, ch, step):
        buf = panels[s * CHUNKS + ch]
        remote(buf.at[row + step], buf.at[row + step], z_send.at[s, ch, 0],
               z_recv.at[s, ch, row + step], to(col, row)).wait_recv()

    def y_copy(s, ch, way):
        buf, source = panels[s * CHUNKS + ch], source_of(way)
        return remote(buf.at[source], buf.at[source], y_send.at[s, ch],
                      z_recv.at[s, ch, source], to(col, row + way))

    def relay(s, ch):
        for way in ways(s, ch):
            @pl.when(row == source_of(way) + way)
            def _():
                y_copy(s, ch, way).wait_recv()
                y_copy(s, ch, way).start()

    def gathered(s, ch):
        for step in reach[::-1]:
            if s == 0:
                @pl.when(reaches(step))
                def _():
                    for k in range(2):
                        open_wait(ch, k, step)
                continue
            ok = reaches(step)
            for way in ways(s, ch):
                if step == -way:
                    ok = ok & (row != source_of(way) + way)

            @pl.when(ok)
            def _():
                z_wait(s, ch, step)
        if s == 0:
            open_wait(ch, 1, 0)

    def c_copy(s, ch, d):
        return remote(sent.at[s, ch, d - 1], landed.at[s, ch, d - 1], c_send.at[s, ch, d - 1],
                      c_recv.at[s, ch, d - 1], to(shifted(d) * 2 + core, row))

    def out_copies(s, ch):
        begin, size = (ch + 1 - fold) * wide, fold * wide
        span = pl.ds(pl.multiple_of(core * half + begin, size), size)
        src = stage.at[s, :, :, pl.ds(begin, size)]
        keep = pltpu.make_async_copy(src.at[0], out.at[s, 0, 0, :, span], o_loc.at[s, ch])
        give = remote(src.at[1], out.at[s, 0, 0, :, span], o_send.at[s, ch], o_recv.at[s, ch], pair)
        return keep, give

    opened = [
        pltpu.make_async_copy(stage.at[0, 0], out.at[0, 0, 0, :, mine], f_loc.at[1]),
        pltpu.make_async_copy(stage.at[0, 1], out.at[0, 0, 0, :, theirs], f_loc.at[2]),
    ]
    for c in opened:
        c.start()

    def solve(s, ch):
        for d in range(1, chips):
            c_copy(s - 1, ch, d).wait_recv()
        for k in range(2):
            block = dv[s, k]
            right = rv[s - 1, k, :, part(ch)]
            total = own[ch, k]
            for d in range(1, chips):
                total = total + unpack(landed[s - 1, ch, d - 1, k]).astype(jnp.float32)
            rem = right.astype(jnp.float32) - total
            high = rem.astype(jnp.bfloat16)
            low = (rem - high.astype(jnp.float32)).astype(jnp.bfloat16)
            x = jnp.dot(jnp.concatenate([block, block], axis=1),
                        jnp.concatenate([high, low], axis=0),
                        preferred_element_type=jnp.float32).astype(jnp.bfloat16)
            if s < links:
                panels[s * CHUNKS + ch][row, k] = pack(x)
            stage[s, k, :, part(ch)] = x
        if s < links:
            for step in reach:
                @pl.when(goes(s, ch, step))
                def _():
                    z_copy(s, ch, step).start()
        if ch % fold == fold - 1:
            for c in out_copies(s, ch):
                c.start()

    def term(s, ch, other, k):
        buf = panels[s * CHUNKS + ch]
        t = other * 2 + (core if k == 0 else 1 - core)
        left, right = [], []
        for slot, index in ((0, cols), (1, cp)):
            for m in range(slots):
                left.append(fv[s, slot, t, m])
                right.append(unpack(buf[index[s, 0, 0, m, t], slot]))
        return jnp.dot(jnp.concatenate(left, axis=1), jnp.concatenate(right, axis=0),
                       preferred_element_type=jnp.float32)

    def spread(s, ch):
        def one(d):
            other = shifted(d)
            for k in range(2):
                sent[s, ch, d - 1, k] = pack(term(s, ch, other, k).astype(jnp.bfloat16))
            c_copy(s, ch, d).start()

        if chips <= 4:
            for d in range(chips - 1, 0, -1):
                one(d)
        else:
            @pl.loop(1, chips)
            def _(d):
                one(d)
        for k in range(2):
            own[ch, k] = term(s, ch, chip, k)

    items = [(s, ch) for s in range(links) for ch in range(CHUNKS)]
    plan = [(i, 0, i) for i in range(len(items))]
    plan += [(i + LAG, 1, i) for i in range(len(items))]
    plan += [(i - EARLY, 2, i) for i in range(CHUNKS, len(items))]
    for _, what, i in sorted(plan):
        s, ch = items[i]
        if what == 0:
            if i == 0:
                arrived("cols")
                arrived("fac0")
            if i == CHUNKS:
                arrived("fac")
            gathered(s, ch)
            spread(s, ch)
        elif what == 1:
            if i == 0:
                arrived("rhs")
                arrived("diag")
            solve(s + 1, ch)
        else:
            relay(s, ch)

    for c in cross.values():
        c.wait_send()
    for c in opened:
        c.wait()
    for ch in range(CHUNKS):
        for step in reach:
            @pl.when(reaches(step))
            def _():
                for k in range(2):
                    open_copy(ch, k, step).wait_send()
        open_copy(ch, 1, 0).wait_send()
    for s in range(steps):
        for ch in range(CHUNKS):
            if s > 0 and ch % fold == fold - 1:
                keep, give = out_copies(s, ch)
                keep.wait()
                give.wait()
            if 0 < s < links:
                for step in reach:
                    @pl.when(goes(s, ch, step))
                    def _():
                        z_copy(s, ch, step).wait_send()
                for way in ways(s, ch):
                    @pl.when(row == source_of(way) + way)
                    def _():
                        y_copy(s, ch, way).wait_send()
            if s < links:
                for d in range(1, chips):
                    c_copy(s, ch, d).wait_send()


def on_device(n_col, n_row, rhs, diag_inv, factor, columns):
    steps, rows, width = rhs.shape[0], rhs.shape[3], rhs.shape[4]
    columns = jnp.swapaxes(columns, 3, 4)
    targets, slots = factor.shape[3], factor.shape[4]
    chips, half = n_col // 2, width // 2
    wide, links = half // CHUNKS, steps - 1
    fold = max(1, 128 // wide)
    packed = (rows // fold, wide * fold)
    bf16 = jnp.bfloat16
    dma = pltpu.SemaphoreType.DMA
    scratch = [
        pltpu.VMEM((2, rows, half), bf16),
        pltpu.VMEM((CHUNKS,) + packed, bf16),
        pltpu.VMEM((links, 2, rows, half), bf16),
        pltpu.VMEM((steps, 2, rows, rows), bf16),
        pltpu.VMEM((links, 2, targets, slots, rows, rows), bf16),
        pltpu.SMEM(columns.shape, jnp.int32),
        pltpu.VMEM((CHUNKS, 2, rows, wide), jnp.float32),
        pltpu.VMEM((links, CHUNKS, chips - 1, 2) + packed, bf16),
        pltpu.VMEM((links, CHUNKS, chips - 1, 2) + packed, bf16),
        pltpu.VMEM((steps, 2, rows, half), bf16),
        dma((3,)), dma((4,)), dma((5,)), dma((5,)),
        dma((CHUNKS, 2, 2 * n_row - 1)), dma((CHUNKS, 2, n_row)),
        dma((links, CHUNKS, 2 * n_row - 1)), dma((links, CHUNKS, n_row)), dma((links, CHUNKS)),
        dma((links, CHUNKS, chips - 1)), dma((links, CHUNKS, chips - 1)),
        dma((steps, CHUNKS)), dma((steps, CHUNKS)), dma((steps, CHUNKS)),
    ] + [pltpu.VMEM((n_row, 2) + packed, bf16) for _ in range(links * CHUNKS)]
    anywhere = pl.BlockSpec(memory_space=pl.ANY)
    return pl.pallas_call(
        functools.partial(kernel, n_col, n_row),
        out_shape=jax.ShapeDtypeStruct(rhs.shape, bf16),
        in_specs=[anywhere, anywhere, anywhere, pl.BlockSpec(memory_space=pltpu.SMEM), anywhere],
        out_specs=anywhere,
        scratch_shapes=scratch,
        compiler_params=pltpu.CompilerParams(
            collective_id=0, has_side_effects=True, vmem_limit_bytes=60 * 1024 * 1024),
        name="levels",
    )(rhs, diag_inv, factor, columns, columns)


def solution(mesh):
    n_col, n_row = mesh.shape["col"], mesh.shape["row"]
    return jax.shard_map(
        functools.partial(on_device, n_col, n_row),
        mesh=mesh,
        in_specs=(
            P(None, "col", "row", None, None),
            P(None, "col", "row", None, None),
            P(None, "col", "row", None, None, None, None),
            P(None, "col", "row", None, None),
        ),
        out_specs=P(None, "col", "row", None, None),
        check_vma=False,
    )
```
